32 devices in a mesh: gx: 4 (over y, core), gy: 8 (over z, x).
Axes of the slice: x: 2, y: 2, z: 4, core: 2. Of those that a mesh axis runs over, the one named last changes fastest.
Arguments:
- tokens: bfloat16 [256, 8192], P('gy', 'gx'), may hold values from -12 to 12
- w_gate: bfloat16 [8192, 28672], P('gx', 'gy'), may hold values from -0.0625 to 0.0625
- w_up: bfloat16 [8192, 28672], P('gx', 'gy'), may hold values from -0.0625 to 0.0625
- w_down: bfloat16 [28672, 8192], P('gy', 'gx'), may hold values from -0.03125 to 0.03125
- w_head: bfloat16 [8192, 1024], P('gx'), may hold values from -0.0625 to 0.0625
- partner: int32 [256], replicated, may hold values from 0 to 255, as said below
Outputs:
- block_out: bfloat16 [256, 8192], P('gy', 'gx')
- pair_loss: float32 [], replicated
- grad_gate: bfloat16 [8192, 28672], P('gx', 'gy')
- grad_up: bfloat16 [8192, 28672], P('gx', 'gy')
- grad_down: bfloat16 [28672, 8192], P('gy', 'gx')
- grad_head: bfloat16 [8192, 1024], P('gx', 'gy')
The draws below stay inside these ranges and needn't reach their ends.
Inputs may be any that keep to these rules, and one draw needn't show every extreme that they name: partner[i] differs from i, and every token is the partner of exactly one token.
All inputs are finite; a program needn't handle non-finite values.
Results may differ from the reference program's by a relative error of at most 0.029.
Values may be sent and summed in bfloat16 or wider, within the bound.
A program may use at most 256 MiB of HBM per device.

```python
import math
import jax
import jax.numpy as jnp
from jax import lax

D = 8192
FF = 28672
E = 1024
TOKENS = 256


def draw_tokens(key, part):
    base = jnp.clip(jax.random.normal(jax.random.fold_in(key, 11), (TOKENS, D), jnp.float32), -6.0, 6.0)
    return base.astype(jnp.bfloat16)


def draw_partner(key, part):
    order = jax.random.permutation(jax.random.fold_in(key, 7), TOKENS).astype(jnp.int32)
    following = jnp.roll(order, -1)
    return jnp.zeros((TOKENS,), jnp.int32).at[order].set(following).astype(jnp.int32)


def shard_levels(rng, extent, cuts, smallest, high):
    factor_of, own = 1.0, jax.random.fold_in(rng, 6)
    for axis_at, shards_of in cuts:
        heights = jnp.exp(jax.random.uniform(jax.random.fold_in(own, axis_at), (shards_of,), jnp.float32, smallest / len(cuts), high / len(cuts)))
        factor_of = factor_of * jnp.repeat(heights, extent[axis_at] // shards_of).reshape([-1 if axis == axis_at else 1 for axis in range(len(extent))])
    return factor_of


def centred(rng, shape, deviation, limit, cuts=(), held_as=jnp.bfloat16):
    factor_of = shard_levels(rng, shape, cuts, -0.22, 0.18) if cuts else 1.0
    result = jax.random.normal(rng, shape, jnp.float32) * deviation * factor_of
    return jnp.minimum(jnp.maximum(result, -limit), limit).astype(held_as)


def setup_inputs(seed: int = 0) -> dict:
    splits = jax.random.split(jax.random.key(seed), 7)
    tokens = draw_tokens(jax.random.fold_in(splits[6], 71), 0)
    w_gate = centred(splits[1], (D, FF), D ** -0.5, 0.0625, ((0, 4), (1, 8)))
    w_up = centred(splits[2], (D, FF), D ** -0.5, 0.0625, ((0, 4), (1, 8)))
    w_down = centred(splits[3], (FF, D), FF ** -0.5, 0.03125, ((0, 8), (1, 4)))
    w_head = centred(splits[4], (D, E), D ** -0.5, 0.0625, ((0, 4),))
    partner = draw_partner(jax.random.fold_in(splits[6], 71), 0)
    return {"tokens": tokens, "w_gate": w_gate, "w_up": w_up, "w_down": w_down, "w_head": w_head, "partner": partner}


def reference(tokens, w_gate, w_up, w_down, w_head, partner):
    token_count = tokens.shape[0]
    score_scale = 1.0 / math.sqrt(E)
    gate_pre = jnp.dot(tokens, w_gate, preferred_element_type=jnp.float32)
    up_pre = jnp.dot(tokens, w_up, preferred_element_type=jnp.float32)
    sigmoid_gate = jax.nn.sigmoid(gate_pre)
    silu_gate = gate_pre * sigmoid_gate
    hidden = (silu_gate * up_pre).astype(jnp.bfloat16)
    block_out = (tokens.astype(jnp.float32) + jnp.dot(hidden, w_down, preferred_element_type=jnp.float32)).astype(jnp.bfloat16)
    projected = jnp.dot(block_out, w_head, preferred_element_type=jnp.float32).astype(jnp.bfloat16)
    scores = jnp.dot(projected, projected.T, preferred_element_type=jnp.float32) * score_scale
    indices = jnp.arange(token_count, dtype=jnp.int32)
    scores = jnp.where(indices[:, None] == indices[None, :], -jnp.inf, scores)
    row_max = lax.optimization_barrier(jnp.max(scores, axis=1, keepdims=True))
    log_total = row_max[:, 0] + jnp.log(lax.optimization_barrier(jnp.sum(jnp.exp(scores - row_max), axis=1)))
    is_partner = indices[None, :] == partner[:, None]
    positive = lax.optimization_barrier(jnp.sum(jnp.where(is_partner, scores, 0.0), axis=1))
    pair_loss = jnp.sum(log_total - positive) / token_count
    weights_grad = (jnp.exp(scores - log_total[:, None]) - is_partner.astype(jnp.float32)).astype(jnp.bfloat16)
    grad_proj = ((jnp.dot(weights_grad, projected, preferred_element_type=jnp.float32) + jnp.dot(weights_grad.T, projected, preferred_element_type=jnp.float32)) * score_scale).astype(jnp.bfloat16)
    grad_block = jnp.dot(grad_proj, w_head.T, preferred_element_type=jnp.float32).astype(jnp.bfloat16)
    grad_head = jnp.dot(block_out.T, grad_proj, preferred_element_type=jnp.float32).astype(jnp.bfloat16)
    grad_down = jnp.dot(hidden.T, grad_block, preferred_element_type=jnp.float32).astype(jnp.bfloat16)
    grad_hidden = jnp.dot(grad_block, w_down.T, preferred_element_type=jnp.float32)
    grad_gate_pre = (grad_hidden * up_pre * sigmoid_gate * (1.0 + gate_pre * (1.0 - sigmoid_gate))).astype(jnp.bfloat16)
    grad_up_pre = (grad_hidden * silu_gate).astype(jnp.bfloat16)
    grad_gate = jnp.dot(tokens.T, grad_gate_pre, preferred_element_type=jnp.float32).astype(jnp.bfloat16)
    grad_up = jnp.dot(tokens.T, grad_up_pre, preferred_element_type=jnp.float32).astype(jnp.bfloat16)
    return (block_out, pair_loss, grad_gate, grad_up, grad_down, grad_head)
```

```python
import functools
import math

import jax
import jax.numpy as jnp
from jax import lax
from jax.experimental import pallas as pl
from jax.experimental.pallas import tpu as pltpu
from jax.sharding import PartitionSpec as P

F32 = jnp.float32
BF16 = jnp.bfloat16
ANY = pl.BlockSpec(memory_space=pl.ANY)
VM = pl.BlockSpec(memory_space=pltpu.VMEM)


def contract_lead(left_mat, right_mat):
    return lax.dot_general(
        left_mat, right_mat, (((0,), (0,)), ((), ())), preferred_element_type=F32
    )


def contract_last(left_mat, right_mat):
    return lax.dot_general(
        left_mat, right_mat, (((1,), (1,)), ((), ())), preferred_element_type=F32
    )


def remote(src, dst, send_sem, recv_sem, device):
    return pltpu.make_async_remote_copy(
        src_ref=src,
        dst_ref=dst,
        send_sem=send_sem,
        recv_sem=recv_sem,
        device_id=device,
        device_id_type=pl.DeviceIdType.MESH,
    )


def span(index, size):
    return pl.ds(pl.multiple_of(index * size, size), size)


def enter(gx, gy):
    ix, iy = lax.axis_index("gx"), lax.axis_index("gy")
    barrier = pltpu.get_barrier_semaphore()
    for o in range(1, gx):
        pl.semaphore_signal(
            barrier, inc=1, device_id={"gx": lax.rem(ix + o, gx)}, device_id_type=pl.DeviceIdType.MESH
        )
    for o in range(1, gy):
        pl.semaphore_signal(
            barrier, inc=1, device_id={"gy": lax.rem(iy + o, gy)}, device_id_type=pl.DeviceIdType.MESH
        )
    pl.semaphore_wait(barrier, gx + gy - 2)
    return ix, iy


class Reduce:
    def __init__(self, gx, rows, chunk, ix, refs, sems, gathered):
        self.pairs = gx // 2
        self.half, self.rows, self.chunk = rows // 2, rows // gx, chunk
        self.core = lax.rem(ix, 2)
        self.pair = lax.div(ix, 2)
        self.part, self.snd1, self.rcv1, self.own2, self.snd2, self.rcv2 = refs
        self.s1, self.r1, self.s2, self.r2, self.s3, self.r3, self.s4, self.r4 = sems
        self.out = gathered
        self.mate = {"gx": self.pair * 2 + 1 - self.core}

    def ahead(self, o):
        return lax.rem(self.pair + o, self.pairs)

    def behind(self, o):
        return lax.rem(self.pair + self.pairs - o, self.pairs)

    def peer(self, o):
        return {"gx": self.ahead(o) * 2 + self.core}

    def block(self, core, pair, c):
        at = span(core * self.pairs + pair, self.rows)
        return self.out.at[:, at, span(c, self.chunk)]

    def hop1(self, c):
        return remote(self.snd1.at[c], self.rcv1.at[c], self.s1.at[c], self.r1.at[c], self.mate)

    def hop2(self, c, o):
        return remote(
            self.snd2.at[c, o - 1], self.rcv2.at[c, o - 1],
            self.s2.at[c, o - 1], self.r2.at[c, o - 1], self.peer(o),
        )

    def hop3(self, c, o, pair):
        at = self.block(self.core, pair, c)
        return remote(at, at, self.s3.at[c, o - 1], self.r3.at[c, o - 1], self.peer(o))

    def hop4(self, c, o, core, pair):
        at = self.block(core, pair, c)
        return remote(at, at, self.s4.at[c, o], self.r4.at[c, o], self.mate)

    def send_partials(self, c):
        slot = lax.rem(c, 2)
        self.snd1[c] = self.part[slot, :, span(1 - self.core, self.half), :].astype(BF16)
        self.hop1(c).start()

    def sum_cores(self, c):
        slot = lax.rem(c, 2)
        self.hop1(c).wait_recv()
        for o in list(range(1, self.pairs)) + [0]:
            at = self.ahead(o)
            total = (
                self.part[slot, :, span(self.core * self.pairs + at, self.rows), :]
                + self.rcv1[c, :, span(at, self.rows), :].astype(F32)
            )
            if o:
                self.snd2[c, o - 1] = total.astype(BF16)
                self.hop2(c, o).start()
            else:
                self.own2[slot] = total

    def sum_pairs(self, c):
        total = self.own2[lax.rem(c, 2)]
        for o in range(1, self.pairs):
            self.hop2(c, o).wait_recv()
            total = total + self.rcv2[c, o - 1].astype(F32)
        return total

    def send_block(self, c, values):
        at = span(self.core * self.pairs + self.pair, self.rows)
        self.out[:, at, span(c, self.chunk)] = values
        for o in range(1, self.pairs):
            self.hop3(c, o, self.pair).start()
        self.hop4(c, 0, self.core, self.pair).start()

    def forward(self, c):
        for o in range(1, self.pairs):
            self.hop3(c, o, self.behind(o)).wait_recv()
            self.hop4(c, o, self.core, self.behind(o)).start()

    def arrived(self, c):
        for o in range(self.pairs):
            self.hop4(c, o, 1 - self.core, self.behind(o)).wait_recv()

    def drain(self, c):
        self.hop1(c).wait_send()
        for o in range(1, self.pairs):
            self.hop2(c, o).wait_send()
            self.hop3(c, o, self.pair).wait_send()
        for o in range(self.pairs):
            self.hop4(c, o, self.core, self.behind(o)).wait_send()

    @staticmethod
    def scratch(gx, rows, chunk, count, summed):
        pairs = gx // 2
        dma = pltpu.SemaphoreType.DMA
        far = max(pairs - 1, 1)
        return [
            pltpu.VMEM((2, summed, rows, chunk), F32),
            pltpu.VMEM((count, summed, rows // 2, chunk), BF16),
            pltpu.VMEM((count, summed, rows // 2, chunk), BF16),
            pltpu.VMEM((2, summed, rows // gx, chunk), F32),
            pltpu.VMEM((count, far, summed, rows // gx, chunk), BF16),
            pltpu.VMEM((count, far, summed, rows // gx, chunk), BF16),
        ], [
            dma((count,)), dma((count,)),
            dma((count, far)), dma((count, far)),
            dma((count, far)), dma((count, far)),
            dma((count, pairs)), dma((count, pairs)),
        ]


def when_chunk(c, count, body):
    @pl.when(jnp.logical_and(c >= 0, c < count))
    def _():
        body(c)


def forward_kernel(
    gx, gy, near, count,
    tok, w_gate, w_up, w_down, w_head,
    rows_out, gate_up_out, hidden_out, block_out, proj_out,
    rows, gate_up, hidden, block, proj, w_in, w_out, w_proj, acc, parts,
    part, snd1, rcv1, own2, snd2, rcv2,
    d_snd, d_rcv, d_snd2, d_rcv2, p_snd, p_rcv,
    s1, r1, s2, r2, s3, r3, s4, r4,
    tz_s, tz_r, tx_s, tx_r, da_s, da_r, db_s, db_r, pa_s, pa_r, pb_s, pb_r, pc_s, pc_r,
    in_sem, out_sem, head_sem, store_sem,
):
    share, width = tok.shape
    far = gy // near
    chunk = w_out.shape[1]
    head = w_head.shape[1] // 2

    def load_in(c):
        slot = lax.rem(c, 2)
        return [
            pltpu.make_async_copy(w.at[:, span(c, chunk)], w_in.at[slot, a], in_sem.at[slot, a])
            for a, w in enumerate((w_gate, w_up))
        ]

    def load_out(c):
        slot = lax.rem(c, 2)
        return pltpu.make_async_copy(w_down.at[span(c, chunk), :], w_out.at[slot], out_sem.at[slot])

    for copy in load_in(jnp.int32(0)):
        copy.start()
    load_head = pltpu.make_async_copy(w_head, w_proj, head_sem.at[0])
    load_out(jnp.int32(0)).start()
    ix, iy = enter(gx, gy)
    fz, nx = lax.div(iy, near), lax.rem(iy, near)

    def gy_at(o, p):
        return lax.rem(fz + o + far, far) * near + lax.rem(nx + p + near, near)

    def token_far(o, source):
        at = rows.at[span(source, share), :]
        return remote(at, at, tz_s.at[o - 1], tz_r.at[o - 1], {"gy": gy_at(o, 0)})

    def token_near(o, p, source):
        at = rows.at[span(source, share), :]
        return remote(at, at, tx_s.at[o, p - 1], tx_r.at[o, p - 1], {"gy": gy_at(0, p)})

    rows[span(iy, share), :] = tok[...]
    for o in range(1, far):
        token_far(o, iy).start()
    for p in range(1, near):
        token_near(0, p, iy).start()
    load_head.start()
    for o in range(1, far):
        token_far(o, gy_at(-o, 0)).wait_recv()
        for p in range(1, near):
            token_near(o, p, gy_at(-o, 0)).start()
    for o in range(far):
        for p in range(1, near):
            token_near(o, p, gy_at(-o, -p)).wait_recv()
    stores = [pltpu.make_async_copy(rows, rows_out, store_sem.at[0])]
    stores[0].start()

    acc[...] = jnp.zeros_like(acc)
    red = Reduce(
        gx, rows.shape[0], chunk, ix, (part, snd1, rcv1, own2, snd2, rcv2),
        (s1, r1, s2, r2, s3, r3, s4, r4), hidden,
    )

    def project_in(c):
        slot = lax.rem(c, 2)
        for copy in load_in(c):
            copy.wait()

        @pl.when(c + 1 < count)
        def _():
            for copy in load_in(c + 1):
                copy.start()

        for a in range(2):
            part[slot, a] = jnp.dot(rows[...], w_in[slot, a], preferred_element_type=F32)
        red.send_partials(c)

    def make_hidden(c):
        total = red.sum_pairs(c)
        gate_up[:, :, span(c, chunk)] = total
        gate, up = total[0], total[1]
        red.send_block(c, (gate * jax.nn.sigmoid(gate) * up).astype(BF16)[None])

    def project_out(c):
        slot = lax.rem(c, 2)
        red.arrived(c)
        load_out(c).wait()

        @pl.when(c + 1 < count)
        def _():
            load_out(c + 1).start()

        acc[...] += jnp.dot(
            hidden[0, :, span(c, chunk)], w_out[slot], preferred_element_type=F32
        )

    def step(s, carry):
        when_chunk(s - 1, count, red.sum_cores)
        when_chunk(s - 2, count, make_hidden)
        when_chunk(s - 3, count, red.forward)
        when_chunk(s, count, project_in)
        when_chunk(s - 4, count, project_out)
        return carry

    lax.fori_loop(0, count + 4, step, 0)
    stores.append(pltpu.make_async_copy(gate_up, gate_up_out, store_sem.at[1]))
    stores.append(pltpu.make_async_copy(hidden, hidden_out, store_sem.at[2]))
    stores[1].start()
    stores[2].start()

    def down_near(o, p):
        return remote(
            d_snd.at[o, p - 1], d_rcv.at[o, p - 1], da_s.at[o, p - 1], da_r.at[o, p - 1],
            {"gy": gy_at(0, p)},
        )

    def down_far(o):
        return remote(
            d_snd2.at[o - 1], d_rcv2.at[o - 1], db_s.at[o - 1], db_r.at[o - 1], {"gy": gy_at(o, 0)}
        )

    order = list(range(1, far)) + [0]
    for o in order:
        for p in range(1, near):
            d_snd[o, p - 1] = acc[span(gy_at(o, p), share), :].astype(BF16)
            down_near(o, p).start()
    total = None
    for o in order:
        total = acc[span(gy_at(o, 0), share), :]
        for p in range(1, near):
            down_near(o, p).wait_recv()
            total = total + d_rcv[o, p - 1].astype(F32)
        if o:
            d_snd2[o - 1] = total.astype(BF16)
            down_far(o).start()
    for o in range(1, far):
        down_far(o).wait_recv()
        total = total + d_rcv2[o - 1].astype(F32)
    block[...] = (tok[...].astype(F32) + total).astype(BF16)
    stores.append(pltpu.make_async_copy(block, block_out, store_sem.at[3]))
    stores[3].start()

    load_head.wait()
    core = red.core
    for h in range(2):
        parts[h] = jnp.dot(
            block[...], w_proj[:, h * head:(h + 1) * head], preferred_element_type=F32
        )

    def head_sum(o):
        return remote(
            p_snd.at[o - 1], p_rcv.at[o - 1], pa_s.at[o - 1], pa_r.at[o - 1],
            {"gx": lax.rem(ix + o, gx)},
        )

    def head_rows(o, source):
        at = proj.at[core, span(source, share), :]
        return remote(at, at, pb_s.at[o - 1], pb_r.at[o - 1], {"gy": lax.rem(iy + o, gy)})

    def head_mate(o, half, source):
        at = proj.at[half, span(source, share), :]
        return remote(at, at, pc_s.at[o], pc_r.at[o], red.mate)

    for o in range(1, gx):
        p_snd[o - 1] = parts[lax.rem(ix + o, 2)].astype(BF16)
        head_sum(o).start()
    total = parts[core]
    for o in range(1, gx):
        head_sum(o).wait_recv()
        total = total + p_rcv[o - 1].astype(F32)
    proj[core, span(iy, share), :] = total.astype(BF16)
    for o in range(1, gy):
        head_rows(o, iy).start()
    head_mate(0, core, iy).start()
    for o in range(1, gy):
        source = lax.rem(iy + gy - o, gy)
        head_rows(o, source).wait_recv()
        head_mate(o, core, source).start()
    for o in range(gy):
        head_mate(o, 1 - core, lax.rem(iy + gy - o, gy)).wait_recv()
    for h in range(2):
        stores.append(
            pltpu.make_async_copy(
                proj.at[h], proj_out.at[:, h * head:(h + 1) * head], store_sem.at[4 + h]
            )
        )
        stores[4 + h].start()

    def finish(c, carry):
        red.drain(c)
        return carry

    lax.fori_loop(0, count, finish, 0)
    for o in range(1, far):
        token_far(o, iy).wait_send()
        down_far(o).wait_send()
    for o in range(far):
        for p in range(1, near):
            token_near(o, p, gy_at(-o, 0)).wait_send()
            down_near(o, p).wait_send()
    for o in range(1, gx):
        head_sum(o).wait_send()
    for o in range(1, gy):
        head_rows(o, iy).wait_send()
    for o in range(gy):
        head_mate(o, core, lax.rem(iy + gy - o, gy)).wait_send()
    for copy in stores:
        copy.wait()


def backward_kernel(
    gx, gy, count,
    grad_block, block, w_down, gate_up,
    grads_out, blocks_out,
    grads, blocks, w_in,
    part, snd1, rcv1, own2, snd2, rcv2,
    s1, r1, s2, r2, s3, r3, s4, r4,
    b_s, b_r, in_sem, store_sem,
):
    share = block.shape[0]
    chunk = w_in.shape[1]

    def load_in(c):
        slot = lax.rem(c, 2)
        return pltpu.make_async_copy(w_down.at[span(c, chunk), :], w_in.at[slot], in_sem.at[slot])

    load_in(jnp.int32(0)).start()
    ix, iy = enter(gx, gy)
    red = Reduce(
        gx, grad_block.shape[0], chunk, ix, (part, snd1, rcv1, own2, snd2, rcv2),
        (s1, r1, s2, r2, s3, r3, s4, r4), grads,
    )

    def share_block(o, source):
        at = blocks.at[span(source, share), :]
        return remote(at, at, b_s.at[o - 1], b_r.at[o - 1], {"gy": lax.rem(iy + o, gy)})

    blocks[span(iy, share), :] = block[...]
    for o in range(1, gy):
        share_block(o, iy).start()

    def project(c):
        slot = lax.rem(c, 2)
        load_in(c).wait()

        @pl.when(c + 1 < count)
        def _():
            load_in(c + 1).start()

        part[slot, 0] = contract_last(grad_block[...], w_in[slot])
        red.send_partials(c)

    def make_grads(c):
        grad_hidden = red.sum_pairs(c)[0]
        gate = gate_up[0, :, span(c, chunk)]
        up = gate_up[1, :, span(c, chunk)]
        sig = jax.nn.sigmoid(gate)
        grad_gate = grad_hidden * up * sig * (1.0 + gate * (1.0 - sig))
        grad_up = grad_hidden * gate * sig
        red.send_block(c, jnp.stack([grad_gate.astype(BF16), grad_up.astype(BF16)]))

    def step(s, carry):
        when_chunk(s - 1, count, red.sum_cores)
        when_chunk(s - 2, count, make_grads)
        when_chunk(s - 3, count, red.forward)
        when_chunk(s, count, project)
        return carry

    lax.fori_loop(0, count + 3, step, 0)

    def finish(c, carry):
        red.arrived(c)
        red.drain(c)
        return carry

    lax.fori_loop(0, count, finish, 0)
    first = pltpu.make_async_copy(grads, grads_out, store_sem.at[0])
    first.start()
    for o in range(1, gy):
        share_block(o, lax.rem(iy + gy - o, gy)).wait_recv()
    second = pltpu.make_async_copy(blocks, blocks_out, store_sem.at[1])
    second.start()
    for o in range(1, gy):
        share_block(o, iy).wait_send()
    first.wait()
    second.wait()


def outer_kernel(left, right, out):
    out[...] = contract_lead(left[...], right[...]).astype(BF16)


def outer(left, right, tile):
    rows, height = left.shape
    width = right.shape[1]
    return pl.pallas_call(
        outer_kernel,
        grid=(height // tile,),
        in_specs=[
            pl.BlockSpec((rows, tile), lambda i: (0, i)),
            pl.BlockSpec((rows, width), lambda i: (0, 0)),
        ],
        out_specs=pl.BlockSpec((tile, width), lambda i: (i, 0)),
        out_shape=jax.ShapeDtypeStruct((height, width), BF16),
        compiler_params=pltpu.CompilerParams(vmem_limit_bytes=40 << 20),
        cost_estimate=pl.CostEstimate(
            flops=2 * rows * height * width,
            bytes_accessed=2 * (rows * height + rows * width + height * width),
            transcendentals=0,
        ),
    )(left, right)


def per_device(gx, gy, tokens, w_gate, w_up, w_down, w_head, partner):
    share, width = tokens.shape
    total_rows = share * gy
    hidden_width = w_gate.shape[1]
    head_width = w_head.shape[1]
    near = 1 << (int(math.log2(gy)) // 2)
    far = gy // near
    count = next(c for c in (7, 8, 4, 2, 1) if hidden_width % (128 * c) == 0)
    chunk = hidden_width // count
    own = total_rows // gx
    dma = pltpu.SemaphoreType.DMA
    shape = jax.ShapeDtypeStruct

    buffers, sems = Reduce.scratch(gx, total_rows, chunk, count, 2)
    fm, nm = max(far - 1, 1), max(near - 1, 1)
    rows_all, gate_up, hidden, block_out, proj_all = pl.pallas_call(
        functools.partial(forward_kernel, gx, gy, near, count),
        in_specs=[VM, ANY, ANY, ANY, ANY],
        out_specs=[ANY] * 5,
        out_shape=[
            shape((total_rows, width), BF16),
            shape((2, own, hidden_width), F32),
            shape((1, total_rows, hidden_width), BF16),
            shape((share, width), BF16),
            shape((total_rows, head_width), BF16),
        ],
        scratch_shapes=[
            pltpu.VMEM((total_rows, width), BF16),
            pltpu.VMEM((2, own, hidden_width), F32),
            pltpu.VMEM((1, total_rows, hidden_width), BF16),
            pltpu.VMEM((share, width), BF16),
            pltpu.VMEM((2, total_rows, head_width // 2), BF16),
            pltpu.VMEM((2, 2, width, chunk), BF16),
            pltpu.VMEM((2, chunk, width), BF16),
            pltpu.VMEM((width, head_width), BF16),
            pltpu.VMEM((total_rows, width), F32),
            pltpu.VMEM((2, share, head_width // 2), F32),
            *buffers,
            pltpu.VMEM((far, nm, share, width), BF16),
            pltpu.VMEM((far, nm, share, width), BF16),
            pltpu.VMEM((fm, share, width), BF16),
            pltpu.VMEM((fm, share, width), BF16),
            pltpu.VMEM((gx - 1, share, head_width // 2), BF16),
            pltpu.VMEM((gx - 1, share, head_width // 2), BF16),
            *sems,
            dma((fm,)), dma((fm,)), dma((far, nm)), dma((far, nm)),
            dma((far, nm)), dma((far, nm)), dma((fm,)), dma((fm,)),
            dma((gx - 1,)), dma((gx - 1,)), dma((gy - 1,)), dma((gy - 1,)),
            dma((gy,)), dma((gy,)),
            dma((2, 2)), dma((2,)), dma((1,)), dma((6,)),
        ],
        compiler_params=pltpu.CompilerParams(
            collective_id=0, has_side_effects=True, vmem_limit_bytes=56 << 20
        ),
    )(tokens, w_gate, w_up, w_down, w_head)
    hidden = hidden[0]

    scale = 1.0 / math.sqrt(head_width)
    ids = jnp.arange(total_rows, dtype=jnp.int32)
    scores = contract_last(proj_all, proj_all) * scale
    scores = jnp.where(ids[:, None] == ids[None, :], -jnp.inf, scores)
    row_max = jnp.max(scores, axis=1, keepdims=True)
    log_total = row_max[:, 0] + jnp.log(jnp.sum(jnp.exp(scores - row_max), axis=1))
    is_partner = ids[None, :] == partner[:, None]
    positive = jnp.sum(jnp.where(is_partner, scores, 0.0), axis=1)
    weights = (jnp.exp(scores - log_total[:, None]) - is_partner.astype(F32)).astype(BF16)
    pair_loss = jnp.sum(log_total - positive) / total_rows
    grad_proj = (
        (jnp.dot(weights, proj_all, preferred_element_type=F32) + contract_lead(weights, proj_all))
        * scale
    ).astype(BF16)
    grad_block = contract_last(grad_proj, w_head).astype(BF16)

    buffers, sems = Reduce.scratch(gx, total_rows, chunk, count, 1)
    grads, blocks = pl.pallas_call(
        functools.partial(backward_kernel, gx, gy, count),
        in_specs=[VM, VM, ANY, VM],
        out_specs=[ANY] * 2,
        out_shape=[
            shape((2, total_rows, hidden_width), BF16),
            shape((total_rows, width), BF16),
        ],
        scratch_shapes=[
            pltpu.VMEM((2, total_rows, hidden_width), BF16),
            pltpu.VMEM((total_rows, width), BF16),
            pltpu.VMEM((2, chunk, width), BF16),
            *buffers,
            *sems,
            dma((gy - 1,)), dma((gy - 1,)), dma((2,)), dma((2,)),
        ],
        compiler_params=pltpu.CompilerParams(
            collective_id=1, has_side_effects=True, vmem_limit_bytes=48 << 20
        ),
    )(grad_block, block_out, w_down, gate_up)

    grad_down = outer(hidden, grad_block, 256)
    grad_gate = outer(rows_all, grads[0], 256)
    grad_up = outer(rows_all, grads[1], 256)
    mine = head_width // gy
    proj_mine = lax.dynamic_slice_in_dim(grad_proj, lax.axis_index("gy") * mine, mine, 1)
    grad_head = contract_lead(blocks, proj_mine).astype(BF16)
    return (block_out, pair_loss, grad_gate, grad_up, grad_down, grad_head)


def solution(mesh):
    in_specs = (P("gy", "gx"), P("gx", "gy"), P("gx", "gy"), P("gy", "gx"), P("gx", None), P())
    out_specs = (P("gy", "gx"), P(), P("gx", "gy"), P("gx", "gy"), P("gy", "gx"), P("gx", "gy"))
    body = functools.partial(per_device, mesh.shape["gx"], mesh.shape["gy"])
    return jax.shard_map(body, mesh=mesh, in_specs=in_specs, out_specs=out_specs, check_vma=False)
```

```python
import functools
import math

import jax
import jax.numpy as jnp
from jax import lax
from jax.experimental import pallas as pl
from jax.experimental.pallas import tpu as pltpu
from jax.sharding import PartitionSpec as P

F32 = jnp.float32
BF16 = jnp.bfloat16
ANY = pl.BlockSpec(memory_space=pl.ANY)
VM = pl.BlockSpec(memory_space=pltpu.VMEM)


def contract_lead(left_mat, right_mat):
    return lax.dot_general(
        left_mat, right_mat, (((0,), (0,)), ((), ())), preferred_element_type=F32
    )


def contract_last(left_mat, right_mat):
    return lax.dot_general(
        left_mat, right_mat, (((1,), (1,)), ((), ())), preferred_element_type=F32
    )


def remote(src, dst, send_sem, recv_sem, device):
    return pltpu.make_async_remote_copy(
        src_ref=src,
        dst_ref=dst,
        send_sem=send_sem,
        recv_sem=recv_sem,
        device_id=device,
        device_id_type=pl.DeviceIdType.MESH,
    )


def span(index, size):
    return pl.ds(pl.multiple_of(index * size, size), size)


def enter(gx, gy):
    ix, iy = lax.axis_index("gx"), lax.axis_index("gy")
    barrier = pltpu.get_barrier_semaphore()
    for o in range(1, gx):
        pl.semaphore_signal(
            barrier, inc=1, device_id={"gx": lax.rem(ix + o, gx)}, device_id_type=pl.DeviceIdType.MESH
        )
    for o in range(1, gy):
        pl.semaphore_signal(
            barrier, inc=1, device_id={"gy": lax.rem(iy + o, gy)}, device_id_type=pl.DeviceIdType.MESH
        )
    pl.semaphore_wait(barrier, gx + gy - 2)
    return ix, iy


class Reduce:
    def __init__(self, gx, rows, chunk, ix, refs, sems, gathered):
        self.pairs = gx // 2
        self.half, self.rows, self.chunk = rows // 2, rows // gx, chunk
        self.core = lax.rem(ix, 2)
        self.pair = lax.div(ix, 2)
        self.part, self.snd1, self.rcv1, self.own2, self.snd2, self.rcv2 = refs
        self.s1, self.r1, self.s2, self.r2, self.s3, self.r3, self.s4, self.r4 = sems
        self.out = gathered
        self.mate = {"gx": self.pair * 2 + 1 - self.core}

    def ahead(self, o):
        return lax.rem(self.pair + o, self.pairs)

    def behind(self, o):
        return lax.rem(self.pair + self.pairs - o, self.pairs)

    def peer(self, o):
        return {"gx": self.ahead(o) * 2 + self.core}

    def block(self, core, pair, c):
        at = span(core * self.pairs + pair, self.rows)
        return self.out.at[:, at, span(c, self.chunk)]

    def hop1(self, c):
        return remote(self.snd1.at[c], self.rcv1.at[c], self.s1.at[c], self.r1.at[c], self.mate)

    def hop2(self, c, o):
        return remote(
            self.snd2.at[c, o - 1], self.rcv2.at[c, o - 1],
            self.s2.at[c, o - 1], self.r2.at[c, o - 1], self.peer(o),
        )

    def hop3(self, c, o, pair):
        at = self.block(self.core, pair, c)
        return remote(at, at, self.s3.at[c, o - 1], self.r3.at[c, o - 1], self.peer(o))

    def hop4(self, c, o, core, pair):
        at = self.block(core, pair, c)
        return remote(at, at, self.s4.at[c, o], self.r4.at[c, o], self.mate)

    def send_partials(self, c):
        slot = lax.rem(c, 2)
        self.snd1[c] = self.part[slot, :, span(1 - self.core, self.half), :].astype(BF16)
        self.hop1(c).start()

    def sum_cores(self, c):
        slot = lax.rem(c, 2)
        self.hop1(c).wait_recv()
        for o in list(range(1, self.pairs)) + [0]:
            at = self.ahead(o)
            total = (
                self.part[slot, :, span(self.core * self.pairs + at, self.rows), :]
                + self.rcv1[c, :, span(at, self.rows), :].astype(F32)
            )
            if o:
                self.snd2[c, o - 1] = total.astype(BF16)
                self.hop2(c, o).start()
            else:
                self.own2[slot] = total

    def sum_pairs(self, c):
        total = self.own2[lax.rem(c, 2)]
        for o in range(1, self.pairs):
            self.hop2(c, o).wait_recv()
            total = total + self.rcv2[c, o - 1].astype(F32)
        return total

    def send_block(self, c, values):
        at = span(self.core * self.pairs + self.pair, self.rows)
        self.out[:, at, span(c, self.chunk)] = values
        for o in range(1, self.pairs):
            self.hop3(c, o, self.pair).start()
        self.hop4(c, 0, self.core, self.pair).start()

    def forward(self, c):
        for o in range(1, self.pairs):
            self.hop3(c, o, self.behind(o)).wait_recv()
            self.hop4(c, o, self.core, self.behind(o)).start()

    def arrived(self, c):
        for o in range(self.pairs):
            self.hop4(c, o, 1 - self.core, self.behind(o)).wait_recv()

    def drain(self, c):
        self.hop1(c).wait_send()
        for o in range(1, self.pairs):
            self.hop2(c, o).wait_send()
            self.hop3(c, o, self.pair).wait_send()
        for o in range(self.pairs):
            self.hop4(c, o, self.core, self.behind(o)).wait_send()

    @staticmethod
    def scratch(gx, rows, chunk, count, summed):
        pairs = gx // 2
        dma = pltpu.SemaphoreType.DMA
        far = max(pairs - 1, 1)
        return [
            pltpu.VMEM((2, summed, rows, chunk), F32),
            pltpu.VMEM((count, summed, rows // 2, chunk), BF16),
            pltpu.VMEM((count, summed, rows // 2, chunk), BF16),
            pltpu.VMEM((2, summed, rows // gx, chunk), F32),
            pltpu.VMEM((count, far, summed, rows // gx, chunk), BF16),
            pltpu.VMEM((count, far, summed, rows // gx, chunk), BF16),
        ], [
            dma((count,)), dma((count,)),
            dma((count, far)), dma((count, far)),
            dma((count, far)), dma((count, far)),
            dma((count, pairs)), dma((count, pairs)),
        ]


def when_chunk(c, count, body):
    @pl.when(jnp.logical_and(c >= 0, c < count))
    def _():
        body(c)


def forward_kernel(
    gx, gy, near, count,
    tok, w_gate, w_up, w_down, w_head,
    rows_out, hidden_out, gate_out, up_out, block_out, proj_out,
    rows, factors, hidden, block, proj, w_in, w_out, w_proj, acc, parts,
    part, snd1, rcv1, own2, snd2, rcv2,
    d_snd, d_rcv, d_snd2, d_rcv2, p_snd, p_rcv,
    s1, r1, s2, r2, s3, r3, s4, r4,
    tz_s, tz_r, tx_s, tx_r, da_s, da_r, db_s, db_r, pa_s, pa_r, pb_s, pb_r, pc_s, pc_r, fa_s, fa_r, fb_s, fb_r,
    in_sem, out_sem, head_sem, store_sem,
):
    share, width = tok.shape
    far = gy // near
    chunk, deep = w_in.shape[3], w_out.shape[1]
    group = deep // chunk
    head = w_head.shape[1] // 2

    def load_in(c):
        slot = lax.rem(c, 2)
        return [
            pltpu.make_async_copy(w.at[:, span(c, chunk)], w_in.at[slot, a], in_sem.at[slot, a])
            for a, w in enumerate((w_gate, w_up))
        ]

    def load_out(g):
        slot = lax.rem(g, 2)
        return pltpu.make_async_copy(w_down.at[span(g, deep), :], w_out.at[slot], out_sem.at[slot])

    for copy in load_in(jnp.int32(0)):
        copy.start()
    load_head = pltpu.make_async_copy(w_head, w_proj, head_sem.at[0])
    load_out(jnp.int32(0)).start()
    ix, iy = enter(gx, gy)
    fz, nx = lax.div(iy, near), lax.rem(iy, near)

    def gy_at(o, p):
        return lax.rem(fz + o + far, far) * near + lax.rem(nx + p + near, near)

    def token_far(o, source):
        at = rows.at[span(source, share), :]
        return remote(at, at, tz_s.at[o - 1], tz_r.at[o - 1], {"gy": gy_at(o, 0)})

    def token_near(o, p, source):
        at = rows.at[span(source, share), :]
        return remote(at, at, tx_s.at[o, p - 1], tx_r.at[o, p - 1], {"gy": gy_at(0, p)})

    rows[span(iy, share), :] = tok[...]
    for o in range(1, far):
        token_far(o, iy).start()
    for p in range(1, near):
        token_near(0, p, iy).start()
    load_head.start()
    for o in range(1, far):
        token_far(o, gy_at(-o, 0)).wait_recv()
        for p in range(1, near):
            token_near(o, p, gy_at(-o, 0)).start()
    for o in range(far):
        for p in range(1, near):
            token_near(o, p, gy_at(-o, -p)).wait_recv()
    stores = [pltpu.make_async_copy(rows, rows_out, store_sem.at[0])]
    stores[0].start()

    acc[...] = jnp.zeros_like(acc)
    red = Reduce(
        gx, rows.shape[0], chunk, ix, (part, snd1, rcv1, own2, snd2, rcv2),
        (s1, r1, s2, r2, s3, r3, s4, r4), hidden,
    )

    def project_in(c):
        slot = lax.rem(c, 2)
        for copy in load_in(c):
            copy.wait()

        @pl.when(c + 1 < count)
        def _():
            for copy in load_in(c + 1):
                copy.start()

        for a in range(2):
            part[slot, a] = jnp.dot(rows[...], w_in[slot, a], preferred_element_type=F32)
        red.send_partials(c)

    def make_hidden(c):
        total = red.sum_pairs(c)
        gate, up = total[0], total[1]
        sig = jax.nn.sigmoid(gate)
        silu = gate * sig
        red.send_block(c, (silu * up).astype(BF16)[None])
        at = span(red.core * red.pairs + red.pair, red.rows)
        factors[0, at, span(c, chunk)] = (up * sig * (1.0 + gate * (1.0 - sig))).astype(BF16)
        factors[1, at, span(c, chunk)] = silu.astype(BF16)

    def project_out(c):
        red.arrived(c)

        @pl.when(lax.rem(c, group) == group - 1)
        def _():
            g = lax.div(c, group)
            slot = lax.rem(g, 2)
            load_out(g).wait()

            @pl.when(g + 1 < count // group)
            def _():
                load_out(g + 1).start()

            acc[...] += jnp.dot(
                hidden[0, :, span(g, deep)], w_out[slot], preferred_element_type=F32
            )

    def step(s, carry):
        when_chunk(s - 1, count, red.sum_cores)
        when_chunk(s - 2, count, make_hidden)
        when_chunk(s - 3, count, red.forward)
        when_chunk(s, count, project_in)
        when_chunk(s - 4, count, project_out)
        return carry

    lax.fori_loop(0, count + 4, step, 0)
    stores.append(pltpu.make_async_copy(hidden.at[0], hidden_out, store_sem.at[1]))
    stores[1].start()

    def down_near(o, p):
        return remote(
            d_snd.at[o, p - 1], d_rcv.at[o, p - 1], da_s.at[o, p - 1], da_r.at[o, p - 1],
            {"gy": gy_at(0, p)},
        )

    def down_far(o):
        return remote(
            d_snd2.at[o - 1], d_rcv2.at[o - 1], db_s.at[o - 1], db_r.at[o - 1], {"gy": gy_at(o, 0)}
        )

    order = list(range(1, far)) + [0]
    for o in order:
        for p in range(1, near):
            d_snd[o, p - 1] = acc[span(gy_at(o, p), share), :].astype(BF16)
            down_near(o, p).start()

    def factor_pair(o, pair):
        at = factors.at[:, span(red.core * red.pairs + pair, red.rows), :]
        return remote(at, at, fa_s.at[o - 1], fa_r.at[o - 1], red.peer(o))

    def factor_mate(o, core, pair):
        at = factors.at[:, span(core * red.pairs + pair, red.rows), :]
        return remote(at, at, fb_s.at[o], fb_r.at[o], red.mate)

    for o in range(1, red.pairs):
        factor_pair(o, red.pair).start()
    factor_mate(0, red.core, red.pair).start()
    total = None
    for o in order:
        total = acc[span(gy_at(o, 0), share), :]
        for p in range(1, near):
            down_near(o, p).wait_recv()
            total = total + d_rcv[o, p - 1].astype(F32)
        if o:
            d_snd2[o - 1] = total.astype(BF16)
            down_far(o).start()
    for o in range(1, far):
        down_far(o).wait_recv()
        total = total + d_rcv2[o - 1].astype(F32)
    block[...] = (tok[...].astype(F32) + total).astype(BF16)
    stores.append(pltpu.make_async_copy(block, block_out, store_sem.at[2]))
    stores[2].start()

    load_head.wait()
    core = red.core
    for h in range(2):
        parts[h] = jnp.dot(
            block[...], w_proj[:, h * head:(h + 1) * head], preferred_element_type=F32
        )

    def head_sum(o):
        return remote(
            p_snd.at[o - 1], p_rcv.at[o - 1], pa_s.at[o - 1], pa_r.at[o - 1],
            {"gx": lax.rem(ix + o, gx)},
        )

    def head_rows(o, source):
        at = proj.at[core, span(source, share), :]
        return remote(at, at, pb_s.at[o - 1], pb_r.at[o - 1], {"gy": lax.rem(iy + o, gy)})

    def head_mate(o, half, source):
        at = proj.at[half, span(source, share), :]
        return remote(at, at, pc_s.at[o], pc_r.at[o], red.mate)

    for o in range(1, gx):
        p_snd[o - 1] = parts[lax.rem(ix + o, 2)].astype(BF16)
        head_sum(o).start()
    total = parts[core]
    for o in range(1, gx):
        head_sum(o).wait_recv()
        total = total + p_rcv[o - 1].astype(F32)
    proj[core, span(iy, share), :] = total.astype(BF16)
    for o in range(1, gy):
        head_rows(o, iy).start()
    head_mate(0, core, iy).start()
    for o in range(1, gy):
        source = lax.rem(iy + gy - o, gy)
        head_rows(o, source).wait_recv()
        head_mate(o, core, source).start()
    for o in range(gy):
        head_mate(o, 1 - core, lax.rem(iy + gy - o, gy)).wait_recv()
    for h in range(2):
        stores.append(
            pltpu.make_async_copy(
                proj.at[h], proj_out.at[:, h * head:(h + 1) * head], store_sem.at[3 + h]
            )
        )
        stores[3 + h].start()
    for o in range(1, red.pairs):
        factor_pair(o, red.behind(o)).wait_recv()
        factor_mate(o, core, red.behind(o)).start()
    for o in range(red.pairs):
        factor_mate(o, 1 - core, red.behind(o)).wait_recv()
    for a, out in enumerate((gate_out, up_out)):
        stores.append(pltpu.make_async_copy(factors.at[a], out, store_sem.at[5 + a]))
        stores[5 + a].start()

    def finish(c, carry):
        red.drain(c)
        return carry

    lax.fori_loop(0, count, finish, 0)
    for o in range(1, far):
        token_far(o, iy).wait_send()
        down_far(o).wait_send()
    for o in range(far):
        for p in range(1, near):
            token_near(o, p, gy_at(-o, 0)).wait_send()
            down_near(o, p).wait_send()
    for o in range(1, red.pairs):
        factor_pair(o, red.pair).wait_send()
    for o in range(red.pairs):
        factor_mate(o, core, red.behind(o)).wait_send()
    for o in range(1, gx):
        head_sum(o).wait_send()
    for o in range(1, gy):
        head_rows(o, iy).wait_send()
    for o in range(gy):
        head_mate(o, core, lax.rem(iy + gy - o, gy)).wait_send()
    for copy in stores:
        copy.wait()


def backward_kernel(
    gx, gy, count,
    grad_block, block, w_down, gate_in, up_in,
    gate_out, up_out, blocks_out,
    grads, blocks, w_in, factors, results,
    part, snd1, rcv1, own2, snd2, rcv2,
    s1, r1, s2, r2, s3, r3, s4, r4,
    b_s, b_r, in_sem, fac_sem, store_sem,
):
    share = block.shape[0]
    chunk = w_in.shape[1]

    def load_in(c):
        slot = lax.rem(c, 2)
        return pltpu.make_async_copy(w_down.at[span(c, chunk), :], w_in.at[slot], in_sem.at[slot])

    load_in(jnp.int32(0)).start()
    fetch = [
        pltpu.make_async_copy(source, factors.at[a], fac_sem.at[a])
        for a, source in enumerate((gate_in, up_in))
    ]
    for copy in fetch:
        copy.start()
    ix, iy = enter(gx, gy)
    red = Reduce(
        gx, grad_block.shape[0], chunk, ix, (part, snd1, rcv1, own2, snd2, rcv2),
        (s1, r1, s2, r2, s3, r3, s4, r4), grads,
    )

    def share_block(o, source):
        at = blocks.at[span(source, share), :]
        return remote(at, at, b_s.at[o - 1], b_r.at[o - 1], {"gy": lax.rem(iy + o, gy)})

    blocks[span(iy, share), :] = block[...]
    for o in range(1, gy):
        share_block(o, iy).start()

    def project(c):
        slot = lax.rem(c, 2)
        load_in(c).wait()

        @pl.when(c + 1 < count)
        def _():
            load_in(c + 1).start()

        part[slot, 0] = contract_last(grad_block[...], w_in[slot])
        red.send_partials(c)

    def gather(c):
        red.send_block(c, red.sum_pairs(c).astype(BF16))

    def make_grads(c):
        red.arrived(c)
        grad_hidden = grads[0, :, span(c, chunk)].astype(F32)
        for a in range(2):
            results[a, :, span(c, chunk)] = (
                grad_hidden * factors[a, :, span(c, chunk)].astype(F32)
            ).astype(BF16)

    def step(s, carry):
        when_chunk(s - 1, count, red.sum_cores)
        when_chunk(s - 2, count, gather)
        when_chunk(s - 3, count, red.forward)
        when_chunk(s, count, project)
        when_chunk(s - 4, count, make_grads)
        return carry

    for copy in fetch:
        copy.wait()
    lax.fori_loop(0, count + 4, step, 0)
    stores = [
        pltpu.make_async_copy(results.at[a], out, store_sem.at[a])
        for a, out in enumerate((gate_out, up_out))
    ]
    for copy in stores:
        copy.start()

    def finish(c, carry):
        red.drain(c)
        return carry

    lax.fori_loop(0, count, finish, 0)
    for o in range(1, gy):
        share_block(o, lax.rem(iy + gy - o, gy)).wait_recv()
    stores.append(pltpu.make_async_copy(blocks, blocks_out, store_sem.at[2]))
    stores[2].start()
    for o in range(1, gy):
        share_block(o, iy).wait_send()
    for copy in stores:
        copy.wait()


def outer_kernel(left, right, out):
    out[...] = contract_lead(left[...], right[...]).astype(BF16)


def outer(left, right, tile):
    rows, height = left.shape
    width = right.shape[1]
    return pl.pallas_call(
        outer_kernel,
        grid=(height // tile,),
        in_specs=[
            pl.BlockSpec((rows, tile), lambda i: (0, i)),
            pl.BlockSpec((rows, width), lambda i: (0, 0)),
        ],
        out_specs=pl.BlockSpec((tile, width), lambda i: (i, 0)),
        out_shape=jax.ShapeDtypeStruct((height, width), BF16),
        compiler_params=pltpu.CompilerParams(vmem_limit_bytes=40 << 20),
        cost_estimate=pl.CostEstimate(
            flops=2 * rows * height * width,
            bytes_accessed=2 * (rows * height + rows * width + height * width),
            transcendentals=0,
        ),
    )(left, right)


def per_device(gx, gy, tokens, w_gate, w_up, w_down, w_head, partner):
    share, width = tokens.shape
    total_rows = share * gy
    hidden_width = w_gate.shape[1]
    head_width = w_head.shape[1]
    near = 1 << (int(math.log2(gy)) // 2)
    far = gy // near
    count = next(c for c in (14, 16, 8, 4, 2) if hidden_width % (128 * c) == 0)
    chunk = hidden_width // count
    deep = 2 * chunk
    dma = pltpu.SemaphoreType.DMA
    shape = jax.ShapeDtypeStruct

    buffers, sems = Reduce.scratch(gx, total_rows, chunk, count, 2)
    fm, nm, pm = max(far - 1, 1), max(near - 1, 1), max(gx // 2 - 1, 1)
    rows_all, hidden, gate_factor, up_factor, block_out, proj_all = pl.pallas_call(
        functools.partial(forward_kernel, gx, gy, near, count),
        in_specs=[VM, ANY, ANY, ANY, ANY],
        out_specs=[ANY] * 6,
        out_shape=[
            shape((total_rows, width), BF16),
            shape((total_rows, hidden_width), BF16),
            shape((total_rows, hidden_width), BF16),
            shape((total_rows, hidden_width), BF16),
            shape((share, width), BF16),
            shape((total_rows, head_width), BF16),
        ],
        scratch_shapes=[
            pltpu.VMEM((total_rows, width), BF16),
            pltpu.VMEM((2, total_rows, hidden_width), BF16),
            pltpu.VMEM((1, total_rows, hidden_width), BF16),
            pltpu.VMEM((share, width), BF16),
            pltpu.VMEM((2, total_rows, head_width // 2), BF16),
            pltpu.VMEM((2, 2, width, chunk), BF16),
            pltpu.VMEM((2, deep, width), BF16),
            pltpu.VMEM((width, head_width), BF16),
            pltpu.VMEM((total_rows, width), F32),
            pltpu.VMEM((2, share, head_width // 2), F32),
            *buffers,
            pltpu.VMEM((far, nm, share, width), BF16),
            pltpu.VMEM((far, nm, share, width), BF16),
            pltpu.VMEM((fm, share, width), BF16),
            pltpu.VMEM((fm, share, width), BF16),
            pltpu.VMEM((gx - 1, share, head_width // 2), BF16),
            pltpu.VMEM((gx - 1, share, head_width // 2), BF16),
            *sems,
            dma((fm,)), dma((fm,)), dma((far, nm)), dma((far, nm)),
            dma((far, nm)), dma((far, nm)), dma((fm,)), dma((fm,)),
            dma((gx - 1,)), dma((gx - 1,)), dma((gy - 1,)), dma((gy - 1,)),
            dma((gy,)), dma((gy,)),
            dma((pm,)), dma((pm,)), dma((gx // 2,)), dma((gx // 2,)),
            dma((2, 2)), dma((2,)), dma((1,)), dma((7,)),
        ],
        compiler_params=pltpu.CompilerParams(
            collective_id=0, has_side_effects=True, vmem_limit_bytes=56 << 20
        ),
    )(tokens, w_gate, w_up, w_down, w_head)

    scale = 1.0 / math.sqrt(head_width)
    ids = jnp.arange(total_rows, dtype=jnp.int32)
    scores = contract_last(proj_all, proj_all) * scale
    scores = jnp.where(ids[:, None] == ids[None, :], -jnp.inf, scores)
    row_max = jnp.max(scores, axis=1, keepdims=True)
    log_total = row_max[:, 0] + jnp.log(jnp.sum(jnp.exp(scores - row_max), axis=1))
    is_partner = ids[None, :] == partner[:, None]
    positive = jnp.sum(jnp.where(is_partner, scores, 0.0), axis=1)
    weights = (jnp.exp(scores - log_total[:, None]) - is_partner.astype(F32)).astype(BF16)
    pair_loss = jnp.sum(log_total - positive) / total_rows
    grad_proj = (
        (jnp.dot(weights, proj_all, preferred_element_type=F32) + contract_lead(weights, proj_all))
        * scale
    ).astype(BF16)
    grad_block = contract_last(grad_proj, w_head).astype(BF16)

    buffers, sems = Reduce.scratch(gx, total_rows, chunk, count, 1)
    gate_grads, up_grads, blocks = pl.pallas_call(
        functools.partial(backward_kernel, gx, gy, count),
        in_specs=[VM, VM, ANY, ANY, ANY],
        out_specs=[ANY] * 3,
        out_shape=[
            shape((total_rows, hidden_width), BF16),
            shape((total_rows, hidden_width), BF16),
            shape((total_rows, width), BF16),
        ],
        scratch_shapes=[
            pltpu.VMEM((1, total_rows, hidden_width), BF16),
            pltpu.VMEM((total_rows, width), BF16),
            pltpu.VMEM((2, chunk, width), BF16),
            pltpu.VMEM((2, total_rows, hidden_width), BF16),
            pltpu.VMEM((2, total_rows, hidden_width), BF16),
            *buffers,
            *sems,
            dma((gy - 1,)), dma((gy - 1,)), dma((2,)), dma((2,)), dma((3,)),
        ],
        compiler_params=pltpu.CompilerParams(
            collective_id=1, has_side_effects=True, vmem_limit_bytes=48 << 20
        ),
    )(grad_block, block_out, w_down, gate_factor, up_factor)

    grad_down = outer(hidden, grad_block, 256)
    grad_gate = outer(rows_all, gate_grads, 256)
    grad_up = outer(rows_all, up_grads, 256)
    mine = head_width // gy
    proj_mine = lax.dynamic_slice_in_dim(grad_proj, lax.axis_index("gy") * mine, mine, 1)
    grad_head = contract_lead(blocks, proj_mine).astype(BF16)
    return (block_out, pair_loss, grad_gate, grad_up, grad_down, grad_head)


def solution(mesh):
    in_specs = (P("gy", "gx"), P("gx", "gy"), P("gx", "gy"), P("gy", "gx"), P("gx", None), P())
    out_specs = (P("gy", "gx"), P(), P("gx", "gy"), P("gx", "gy"), P("gy", "gx"), P("gx", "gy"))
    body = functools.partial(per_device, mesh.shape["gx"], mesh.shape["gy"])
    return jax.shard_map(body, mesh=mesh, in_specs=in_specs, out_specs=out_specs, check_vma=False)
```

```python
import functools
import math

import jax
import jax.numpy as jnp
from jax import lax
from jax.experimental import pallas as pl
from jax.experimental.pallas import tpu as pltpu
from jax.sharding import PartitionSpec as P

F32 = jnp.float32
BF16 = jnp.bfloat16
ANY = pl.BlockSpec(memory_space=pl.ANY)
VM = pl.BlockSpec(memory_space=pltpu.VMEM)


def contract_lead(left_mat, right_mat):
    return lax.dot_general(
        left_mat, right_mat, (((0,), (0,)), ((), ())), preferred_element_type=F32
    )


def contract_last(left_mat, right_mat):
    return lax.dot_general(
        left_mat, right_mat, (((1,), (1,)), ((), ())), preferred_element_type=F32
    )


def remote(src, dst, send_sem, recv_sem, device):
    return pltpu.make_async_remote_copy(
        src_ref=src,
        dst_ref=dst,
        send_sem=send_sem,
        recv_sem=recv_sem,
        device_id=device,
        device_id_type=pl.DeviceIdType.MESH,
    )


def span(index, size):
    return pl.ds(pl.multiple_of(index * size, size), size)


def enter(gx, gy):
    ix, iy = lax.axis_index("gx"), lax.axis_index("gy")
    barrier = pltpu.get_barrier_semaphore()
    for o in range(1, gx):
        pl.semaphore_signal(
            barrier, inc=1, device_id={"gx": lax.rem(ix + o, gx)}, device_id_type=pl.DeviceIdType.MESH
        )
    for o in range(1, gy):
        pl.semaphore_signal(
            barrier, inc=1, device_id={"gy": lax.rem(iy + o, gy)}, device_id_type=pl.DeviceIdType.MESH
        )
    pl.semaphore_wait(barrier, gx + gy - 2)
    return ix, iy


class Reduce:
    def __init__(self, gx, rows, chunk, ix, refs, sems, gathered):
        self.pairs = gx // 2
        self.half, self.rows, self.chunk = rows // 2, rows // gx, chunk
        self.core = lax.rem(ix, 2)
        self.pair = lax.div(ix, 2)
        self.part, self.snd1, self.rcv1, self.own2, self.snd2, self.rcv2 = refs
        self.s1, self.r1, self.s2, self.r2, self.s3, self.r3, self.s4, self.r4 = sems
        self.out = gathered
        self.mate = {"gx": self.pair * 2 + 1 - self.core}

    def ahead(self, o):
        return lax.rem(self.pair + o, self.pairs)

    def behind(self, o):
        return lax.rem(self.pair + self.pairs - o, self.pairs)

    def peer(self, o):
        return {"gx": self.ahead(o) * 2 + self.core}

    def block(self, core, pair, c):
        at = span(core * self.pairs + pair, self.rows)
        return self.out.at[:, at, span(c, self.chunk)]

    def hop1(self, c):
        return remote(self.snd1.at[c], self.rcv1.at[c], self.s1.at[c], self.r1.at[c], self.mate)

    def hop2(self, c, o):
        return remote(
            self.snd2.at[c, o - 1], self.rcv2.at[c, o - 1],
            self.s2.at[c, o - 1], self.r2.at[c, o - 1], self.peer(o),
        )

    def hop3(self, c, o, pair):
        at = self.block(self.core, pair, c)
        return remote(at, at, self.s3.at[c, o - 1], self.r3.at[c, o - 1], self.peer(o))

    def hop4(self, c, o, core, pair):
        at = self.block(core, pair, c)
        return remote(at, at, self.s4.at[c, o], self.r4.at[c, o], self.mate)

    def send_partials(self, c):
        slot = lax.rem(c, 2)
        self.snd1[c] = self.part[slot, :, span(1 - self.core, self.half), :].astype(BF16)
        self.hop1(c).start()

    def sum_cores(self, c):
        slot = lax.rem(c, 2)
        self.hop1(c).wait_recv()
        for o in list(range(1, self.pairs)) + [0]:
            at = self.ahead(o)
            total = (
                self.part[slot, :, span(self.core * self.pairs + at, self.rows), :]
                + self.rcv1[c, :, span(at, self.rows), :].astype(F32)
            )
            if o:
                self.snd2[c, o - 1] = total.astype(BF16)
                self.hop2(c, o).start()
            else:
                self.own2[slot] = total

    def sum_pairs(self, c):
        total = self.own2[lax.rem(c, 2)]
        for o in range(1, self.pairs):
            self.hop2(c, o).wait_recv()
            total = total + self.rcv2[c, o - 1].astype(F32)
        return total

    def send_block(self, c, values):
        at = span(self.core * self.pairs + self.pair, self.rows)
        self.out[:, at, span(c, self.chunk)] = values
        for o in range(1, self.pairs):
            self.hop3(c, o, self.pair).start()
        self.hop4(c, 0, self.core, self.pair).start()

    def forward(self, c):
        for o in range(1, self.pairs):
            self.hop3(c, o, self.behind(o)).wait_recv()
            self.hop4(c, o, self.core, self.behind(o)).start()

    def arrived(self, c):
        for o in range(self.pairs):
            self.hop4(c, o, 1 - self.core, self.behind(o)).wait_recv()

    def drain(self, c):
        self.hop1(c).wait_send()
        for o in range(1, self.pairs):
            self.hop2(c, o).wait_send()
            self.hop3(c, o, self.pair).wait_send()
        for o in range(self.pairs):
            self.hop4(c, o, self.core, self.behind(o)).wait_send()

    @staticmethod
    def scratch(gx, rows, chunk, count, summed):
        pairs = gx // 2
        dma = pltpu.SemaphoreType.DMA
        far = max(pairs - 1, 1)
        return [
            pltpu.VMEM((2, summed, rows, chunk), F32),
            pltpu.VMEM((count, summed, rows // 2, chunk), BF16),
            pltpu.VMEM((count, summed, rows // 2, chunk), BF16),
            pltpu.VMEM((2, summed, rows // gx, chunk), F32),
            pltpu.VMEM((count, far, summed, rows // gx, chunk), BF16),
            pltpu.VMEM((count, far, summed, rows // gx, chunk), BF16),
        ], [
            dma((count,)), dma((count,)),
            dma((count, far)), dma((count, far)),
            dma((count, far)), dma((count, far)),
            dma((count, pairs)), dma((count, pairs)),
        ]


def when_chunk(c, count, body):
    @pl.when(jnp.logical_and(c >= 0, c < count))
    def _():
        body(c)


def forward_kernel(
    gx, gy, near, count,
    tok, w_gate, w_up, w_down, w_head,
    rows_out, gate_up_out, hidden_out, block_out, proj_out,
    rows, gate_up, hidden, block, proj, w_in, w_out, w_proj, acc, parts,
    part, snd1, rcv1, own2, snd2, rcv2,
    d_snd, d_rcv, d_snd2, d_rcv2, p_snd, p_rcv,
    s1, r1, s2, r2, s3, r3, s4, r4,
    tz_s, tz_r, tx_s, tx_r, da_s, da_r, db_s, db_r, pa_s, pa_r, pb_s, pb_r, pc_s, pc_r,
    in_sem, out_sem, head_sem, store_sem,
):
    share, width = tok.shape
    far = gy // near
    chunk = w_out.shape[1]
    head = w_head.shape[1] // 2

    def load_in(c):
        slot = lax.rem(c, 2)
        return [
            pltpu.make_async_copy(w.at[:, span(c, chunk)], w_in.at[slot, a], in_sem.at[slot, a])
            for a, w in enumerate((w_gate, w_up))
        ]

    def load_out(c):
        slot = lax.rem(c, 2)
        return pltpu.make_async_copy(w_down.at[span(c, chunk), :], w_out.at[slot], out_sem.at[slot])

    for copy in load_in(jnp.int32(0)):
        copy.start()
    load_head = pltpu.make_async_copy(w_head, w_proj, head_sem.at[0])
    load_out(jnp.int32(0)).start()
    ix, iy = enter(gx, gy)
    fz, nx = lax.div(iy, near), lax.rem(iy, near)

    def gy_at(o, p):
        return lax.rem(fz + o + far, far) * near + lax.rem(nx + p + near, near)

    def token_far(o, source):
        at = rows.at[span(source, share), :]
        return remote(at, at, tz_s.at[o - 1], tz_r.at[o - 1], {"gy": gy_at(o, 0)})

    def token_near(o, p, source):
        at = rows.at[span(source, share), :]
        return remote(at, at, tx_s.at[o, p - 1], tx_r.at[o, p - 1], {"gy": gy_at(0, p)})

    rows[span(iy, share), :] = tok[...]
    for o in range(1, far):
        token_far(o, iy).start()
    for p in range(1, near):
        token_near(0, p, iy).start()
    load_head.start()
    for o in range(1, far):
        token_far(o, gy_at(-o, 0)).wait_recv()
        for p in range(1, near):
            token_near(o, p, gy_at(-o, 0)).start()
    for o in range(far):
        for p in range(1, near):
            token_near(o, p, gy_at(-o, -p)).wait_recv()
    stores = [pltpu.make_async_copy(rows, rows_out, store_sem.at[0])]
    stores[0].start()

    acc[...] = jnp.zeros_like(acc)
    red = Reduce(
        gx, rows.shape[0], chunk, ix, (part, snd1, rcv1, own2, snd2, rcv2),
        (s1, r1, s2, r2, s3, r3, s4, r4), hidden,
    )

    def project_in(c):
        slot = lax.rem(c, 2)
        for copy in load_in(c):
            copy.wait()

        @pl.when(c + 1 < count)
        def _():
            for copy in load_in(c + 1):
                copy.start()

        for a in range(2):
            part[slot, a] = jnp.dot(rows[...], w_in[slot, a], preferred_element_type=F32)
        red.send_partials(c)

    def make_hidden(c):
        total = red.sum_pairs(c)
        gate_up[:, :, span(c, chunk)] = total
        gate, up = total[0], total[1]
        red.send_block(c, (gate * jax.nn.sigmoid(gate) * up).astype(BF16)[None])

    def project_out(c):
        slot = lax.rem(c, 2)
        red.arrived(c)
        load_out(c).wait()

        @pl.when(c + 1 < count)
        def _():
            load_out(c + 1).start()

        acc[...] += jnp.dot(
            hidden[0, :, span(c, chunk)], w_out[slot], preferred_element_type=F32
        )

    def step(s, carry):
        when_chunk(s - 1, count, red.sum_cores)
        when_chunk(s - 2, count, make_hidden)
        when_chunk(s - 3, count, red.forward)
        when_chunk(s, count, project_in)
        when_chunk(s - 4, count, project_out)
        return carry

    lax.fori_loop(0, count + 4, step, 0)
    stores.append(pltpu.make_async_copy(gate_up, gate_up_out, store_sem.at[1]))
    stores.append(pltpu.make_async_copy(hidden, hidden_out, store_sem.at[2]))
    stores[1].start()
    stores[2].start()

    def down_near(o, p):
        return remote(
            d_snd.at[o, p - 1], d_rcv.at[o, p - 1], da_s.at[o, p - 1], da_r.at[o, p - 1],
            {"gy": gy_at(0, p)},
        )

    def down_far(o):
        return remote(
            d_snd2.at[o - 1], d_rcv2.at[o - 1], db_s.at[o - 1], db_r.at[o - 1], {"gy": gy_at(o, 0)}
        )

    order = list(range(1, far)) + [0]
    for o in order:
        for p in range(1, near):
            d_snd[o, p - 1] = acc[span(gy_at(o, p), share), :].astype(BF16)
            down_near(o, p).start()
    total = None
    for o in order:
        total = acc[span(gy_at(o, 0), share), :]
        for p in range(1, near):
            down_near(o, p).wait_recv()
            total = total + d_rcv[o, p - 1].astype(F32)
        if o:
            d_snd2[o - 1] = total.astype(BF16)
            down_far(o).start()
    for o in range(1, far):
        down_far(o).wait_recv()
        total = total + d_rcv2[o - 1].astype(F32)
    block[...] = (tok[...].astype(F32) + total).astype(BF16)
    stores.append(pltpu.make_async_copy(block, block_out, store_sem.at[3]))
    stores[3].start()

    load_head.wait()
    core = red.core
    for h in range(2):
        parts[h] = jnp.dot(
            block[...], w_proj[:, h * head:(h + 1) * head], preferred_element_type=F32
        )

    def head_sum(o):
        return remote(
            p_snd.at[o - 1], p_rcv.at[o - 1], pa_s.at[o - 1], pa_r.at[o - 1],
            {"gx": lax.rem(ix + o, gx)},
        )

    def head_rows(o, source):
        at = proj.at[core, span(source, share), :]
        return remote(at, at, pb_s.at[o - 1], pb_r.at[o - 1], {"gy": lax.rem(iy + o, gy)})

    def head_mate(o, half, source):
        at = proj.at[half, span(source, share), :]
        return remote(at, at, pc_s.at[o], pc_r.at[o], red.mate)

    for o in range(1, gx):
        p_snd[o - 1] = parts[lax.rem(ix + o, 2)].astype(BF16)
        head_sum(o).start()
    total = parts[core]
    for o in range(1, gx):
        head_sum(o).wait_recv()
        total = total + p_rcv[o - 1].astype(F32)
    proj[core, span(iy, share), :] = total.astype(BF16)
    for o in range(1, gy):
        head_rows(o, iy).start()
    head_mate(0, core, iy).start()
    for o in range(1, gy):
        source = lax.rem(iy + gy - o, gy)
        head_rows(o, source).wait_recv()
        head_mate(o, core, source).start()
    for o in range(gy):
        head_mate(o, 1 - core, lax.rem(iy + gy - o, gy)).wait_recv()
    for h in range(2):
        stores.append(
            pltpu.make_async_copy(
                proj.at[h], proj_out.at[:, h * head:(h + 1) * head], store_sem.at[4 + h]
            )
        )
        stores[4 + h].start()

    def finish(c, carry):
        red.drain(c)
        return carry

    lax.fori_loop(0, count, finish, 0)
    for o in range(1, far):
        token_far(o, iy).wait_send()
        down_far(o).wait_send()
    for o in range(far):
        for p in range(1, near):
            token_near(o, p, gy_at(-o, 0)).wait_send()
            down_near(o, p).wait_send()
    for o in range(1, gx):
        head_sum(o).wait_send()
    for o in range(1, gy):
        head_rows(o, iy).wait_send()
    for o in range(gy):
        head_mate(o, core, lax.rem(iy + gy - o, gy)).wait_send()
    for copy in stores:
        copy.wait()


def backward_kernel(
    gx, gy, count,
    grad_block, block, w_down, gate_up,
    gate_out, up_out, blocks_out,
    grads, blocks, w_in,
    part, snd1, rcv1, own2, snd2, rcv2,
    s1, r1, s2, r2, s3, r3, s4, r4,
    b_s, b_r, in_sem, store_sem,
):
    share = block.shape[0]
    chunk = w_in.shape[1]

    def load_in(c):
        slot = lax.rem(c, 2)
        return pltpu.make_async_copy(w_down.at[span(c, chunk), :], w_in.at[slot], in_sem.at[slot])

    load_in(jnp.int32(0)).start()
    ix, iy = enter(gx, gy)
    red = Reduce(
        gx, grad_block.shape[0], chunk, ix, (part, snd1, rcv1, own2, snd2, rcv2),
        (s1, r1, s2, r2, s3, r3, s4, r4), grads,
    )

    def share_block(o, source):
        at = blocks.at[span(source, share), :]
        return remote(at, at, b_s.at[o - 1], b_r.at[o - 1], {"gy": lax.rem(iy + o, gy)})

    blocks[span(iy, share), :] = block[...]
    for o in range(1, gy):
        share_block(o, iy).start()

    def project(c):
        slot = lax.rem(c, 2)
        load_in(c).wait()

        @pl.when(c + 1 < count)
        def _():
            load_in(c + 1).start()

        part[slot, 0] = contract_last(grad_block[...], w_in[slot])
        red.send_partials(c)

    def make_grads(c):
        grad_hidden = red.sum_pairs(c)[0]
        gate = gate_up[0, :, span(c, chunk)]
        up = gate_up[1, :, span(c, chunk)]
        sig = jax.nn.sigmoid(gate)
        grad_gate = grad_hidden * up * sig * (1.0 + gate * (1.0 - sig))
        grad_up = grad_hidden * gate * sig
        red.send_block(c, jnp.stack([grad_gate.astype(BF16), grad_up.astype(BF16)]))

    def step(s, carry):
        when_chunk(s - 1, count, red.sum_cores)
        when_chunk(s - 2, count, make_grads)
        when_chunk(s - 3, count, red.forward)
        when_chunk(s, count, project)
        return carry

    lax.fori_loop(0, count + 3, step, 0)

    def finish(c, carry):
        red.arrived(c)
        red.drain(c)
        return carry

    lax.fori_loop(0, count, finish, 0)
    stores = [
        pltpu.make_async_copy(grads.at[a], out, store_sem.at[a])
        for a, out in enumerate((gate_out, up_out))
    ]
    for copy in stores:
        copy.start()
    for o in range(1, gy):
        share_block(o, lax.rem(iy + gy - o, gy)).wait_recv()
    stores.append(pltpu.make_async_copy(blocks, blocks_out, store_sem.at[2]))
    stores[2].start()
    for o in range(1, gy):
        share_block(o, iy).wait_send()
    for copy in stores:
        copy.wait()


def outer_kernel(left, right, out):
    out[...] = contract_lead(left[...], right[...]).astype(BF16)


def outer(left, right):
    rows, height = left.shape
    width = right.shape[1]
    tile = next(t for t in (512, 256, 128) if height % t == 0)
    return pl.pallas_call(
        outer_kernel,
        grid=(height // tile,),
        in_specs=[
            pl.BlockSpec((rows, tile), lambda i: (0, i)),
            pl.BlockSpec((rows, width), lambda i: (0, 0)),
        ],
        out_specs=pl.BlockSpec((tile, width), lambda i: (i, 0)),
        out_shape=jax.ShapeDtypeStruct((height, width), BF16),
        compiler_params=pltpu.CompilerParams(vmem_limit_bytes=40 << 20),
        cost_estimate=pl.CostEstimate(
            flops=2 * rows * height * width,
            bytes_accessed=2 * (rows * height + rows * width + height * width),
            transcendentals=0,
        ),
    )(left, right)


def per_device(gx, gy, tokens, w_gate, w_up, w_down, w_head, partner):
    share, width = tokens.shape
    total_rows = share * gy
    hidden_width = w_gate.shape[1]
    head_width = w_head.shape[1]
    near = 1 << (int(math.log2(gy)) // 2)
    far = gy // near
    count = next(c for c in (7, 8, 4, 2, 1) if hidden_width % (128 * c) == 0)
    chunk = hidden_width // count
    own = total_rows // gx
    dma = pltpu.SemaphoreType.DMA
    shape = jax.ShapeDtypeStruct

    buffers, sems = Reduce.scratch(gx, total_rows, chunk, count, 2)
    fm, nm = max(far - 1, 1), max(near - 1, 1)
    rows_all, gate_up, hidden, block_out, proj_all = pl.pallas_call(
        functools.partial(forward_kernel, gx, gy, near, count),
        in_specs=[VM, ANY, ANY, ANY, ANY],
        out_specs=[ANY] * 5,
        out_shape=[
            shape((total_rows, width), BF16),
            shape((2, own, hidden_width), F32),
            shape((1, total_rows, hidden_width), BF16),
            shape((share, width), BF16),
            shape((total_rows, head_width), BF16),
        ],
        scratch_shapes=[
            pltpu.VMEM((total_rows, width), BF16),
            pltpu.VMEM((2, own, hidden_width), F32),
            pltpu.VMEM((1, total_rows, hidden_width), BF16),
            pltpu.VMEM((share, width), BF16),
            pltpu.VMEM((2, total_rows, head_width // 2), BF16),
            pltpu.VMEM((2, 2, width, chunk), BF16),
            pltpu.VMEM((2, chunk, width), BF16),
            pltpu.VMEM((width, head_width), BF16),
            pltpu.VMEM((total_rows, width), F32),
            pltpu.VMEM((2, share, head_width // 2), F32),
            *buffers,
            pltpu.VMEM((far, nm, share, width), BF16),
            pltpu.VMEM((far, nm, share, width), BF16),
            pltpu.VMEM((fm, share, width), BF16),
            pltpu.VMEM((fm, share, width), BF16),
            pltpu.VMEM((gx - 1, share, head_width // 2), BF16),
            pltpu.VMEM((gx - 1, share, head_width // 2), BF16),
            *sems,
            dma((fm,)), dma((fm,)), dma((far, nm)), dma((far, nm)),
            dma((far, nm)), dma((far, nm)), dma((fm,)), dma((fm,)),
            dma((gx - 1,)), dma((gx - 1,)), dma((gy - 1,)), dma((gy - 1,)),
            dma((gy,)), dma((gy,)),
            dma((2, 2)), dma((2,)), dma((1,)), dma((6,)),
        ],
        compiler_params=pltpu.CompilerParams(
            collective_id=0, has_side_effects=True, vmem_limit_bytes=56 << 20
        ),
    )(tokens, w_gate, w_up, w_down, w_head)
    hidden = hidden[0]

    scale = 1.0 / math.sqrt(head_width)
    ids = jnp.arange(total_rows, dtype=jnp.int32)
    scores = contract_last(proj_all, proj_all) * scale
    scores = jnp.where(ids[:, None] == ids[None, :], -jnp.inf, scores)
    row_max = jnp.max(scores, axis=1, keepdims=True)
    log_total = row_max[:, 0] + jnp.log(jnp.sum(jnp.exp(scores - row_max), axis=1))
    is_partner = ids[None, :] == partner[:, None]
    positive = jnp.sum(jnp.where(is_partner, scores, 0.0), axis=1)
    weights = (jnp.exp(scores - log_total[:, None]) - is_partner.astype(F32)).astype(BF16)
    pair_loss = jnp.sum(log_total - positive) / total_rows
    grad_proj = (
        (jnp.dot(weights, proj_all, preferred_element_type=F32) + contract_lead(weights, proj_all))
        * scale
    ).astype(BF16)
    grad_block = contract_last(grad_proj, w_head).astype(BF16)

    buffers, sems = Reduce.scratch(gx, total_rows, chunk, count, 1)
    gate_grads, up_grads, blocks = pl.pallas_call(
        functools.partial(backward_kernel, gx, gy, count),
        in_specs=[VM, VM, ANY, VM],
        out_specs=[ANY] * 3,
        out_shape=[
            shape((total_rows, hidden_width), BF16),
            shape((total_rows, hidden_width), BF16),
            shape((total_rows, width), BF16),
        ],
        scratch_shapes=[
            pltpu.VMEM((2, total_rows, hidden_width), BF16),
            pltpu.VMEM((total_rows, width), BF16),
            pltpu.VMEM((2, chunk, width), BF16),
            *buffers,
            *sems,
            dma((gy - 1,)), dma((gy - 1,)), dma((2,)), dma((3,)),
        ],
        compiler_params=pltpu.CompilerParams(
            collective_id=1, has_side_effects=True, vmem_limit_bytes=48 << 20
        ),
    )(grad_block, block_out, w_down, gate_up)

    grad_down = outer(hidden, grad_block)
    grad_gate = outer(rows_all, gate_grads)
    grad_up = outer(rows_all, up_grads)
    mine = head_width // gy
    proj_mine = lax.dynamic_slice_in_dim(grad_proj, lax.axis_index("gy") * mine, mine, 1)
    grad_head = contract_lead(blocks, proj_mine).astype(BF16)
    return (block_out, pair_loss, grad_gate, grad_up, grad_down, grad_head)


def solution(mesh):
    in_specs = (P("gy", "gx"), P("gx", "gy"), P("gx", "gy"), P("gy", "gx"), P("gx", None), P())
    out_specs = (P("gy", "gx"), P(), P("gx", "gy"), P("gx", "gy"), P("gy", "gx"), P("gx", "gy"))
    body = functools.partial(per_device, mesh.shape["gx"], mesh.shape["gy"])
    return jax.shard_map(body, mesh=mesh, in_specs=in_specs, out_specs=out_specs, check_vma=False)
```
